32 devices in a mesh: dp: 8 (over z, y), tensor: 4 (over x, core).
Axes of the slice: x: 2, y: 2, z: 4, core: 2. Of those that a mesh axis runs over, the one named last changes fastest.
Arguments:
- hidden_in: bfloat16 [4096, 768], P(('dp', 'tensor')), may hold values from -6 to 6
- segment_ids: int32 [4096], P('dp'), may hold values from 0 to 127, as said below
- qkv_weight: bfloat16 [768, 3, 768], P(None, None, 'tensor'), may hold values from -2 to 2
- out_weight: bfloat16 [768, 768], P('tensor'), may hold values from -0.875 to 0.875
- norm1_gain: float32 [768], replicated, may hold values from 0.1 to 1.9
- in_weight: bfloat16 [768, 2, 1152], P(None, None, 'tensor'), may hold values from -0.21875 to 0.21875
- down_weight: bfloat16 [1152, 768], P('tensor'), may hold values from -0.1875 to 0.1875
- norm2_gain: float32 [768], replicated, may hold values from 0.1 to 1.9
- cotangent: bfloat16 [4096, 768], P(('dp', 'tensor')), may hold values from -6 to 6
Outputs:
- layer_out: float32 [4096, 768], P(('dp', 'tensor'))
- grad_input: float32 [4096, 768], P(('dp', 'tensor'))
- grad_qkv: float32 [768, 3, 768], P(None, None, 'tensor')
- grad_out: float32 [768, 768], P('tensor')
- grad_norm1: float32 [768], replicated
- grad_in: float32 [768, 2, 1152], P(None, None, 'tensor')
- grad_down: float32 [1152, 768], P('tensor')
- grad_norm2: float32 [768], replicated
The draws below stay inside these ranges and needn't reach their ends.
Inputs may be any that keep to these rules, and one draw needn't show every extreme that they name: `segment_ids`: within each block of 512 tokens the ids start at 0 and rise by one at each new sequence; every sequence starts at a multiple of 4 within its block and has a multiple of 4 tokens, 4 to 512; in some block every sequence has exactly 4 tokens, in another every sequence has exactly 512.
All inputs are finite; a program needn't handle non-finite values.
Results may differ from the reference program's by a relative error of at most 0.013.
Values may be sent and summed in bfloat16 or wider, within the bound.
No kernel may reach another device: no remote copies, remote signals or barrier semaphores. Data moves between devices by JAX's collectives and lax.ppermute only.
A program may use at most 64 MiB of HBM per device.

```python
import jax
import jax.numpy as jnp
from jax import lax

D = 768
HEADS = 12
HD = 64
FF = 1152
TOK_DEV = 512
SEQ_MAX = 512
TOKENS = 4096


def draw_segment_ids(key, part):
    blocks = TOKENS // TOK_DEV
    level_key = jax.random.fold_in(key, 11)
    special_key = jax.random.fold_in(key, 12)
    roll_key = jax.random.fold_in(key, 13)
    dense_key = jax.random.fold_in(key, 14)
    levels = jax.random.randint(level_key, (blocks,), 0, 4)
    periods = jnp.array([2, 8, 32, 128], jnp.int32)[levels]
    special = jax.random.randint(special_key, (), 0, blocks)
    dense = (special + 1 + jax.random.randint(dense_key, (), 0, blocks - 1)) % blocks
    rolls = jax.random.randint(roll_key, (blocks, TOK_DEV), 0, 1 << 20)
    places = jnp.arange(TOK_DEV)
    grid = (places % 4 == 0)[None, :]
    block_index = jnp.arange(blocks)[:, None]
    cuts = jnp.logical_and(grid, rolls % periods[:, None] == 0)
    cuts = jnp.where(block_index == special, False, cuts)
    cuts = jnp.where(block_index == dense, grid, cuts)
    forced = (places % SEQ_MAX == 0)[None, :]
    bounds = jnp.logical_or(forced, cuts).astype(jnp.int32)
    return (jnp.cumsum(bounds, axis=1) - 1).astype(jnp.int32).reshape(-1)


def draw_qkv_weight(key, part):
    features = HEADS * HD
    base = jax.random.normal(jax.random.fold_in(key, 21), (D, 3, features), jnp.float32) / jnp.sqrt(jnp.float32(D))
    return jnp.clip(base, -2.0, 2.0).astype(jnp.bfloat16)


def block_levels(own_key, extent, pieces, low, high):
    level, own = 1.0, jax.random.fold_in(own_key, 6)
    for axis_at, parts in pieces:
        steps = jnp.exp(jax.random.uniform(jax.random.fold_in(own, axis_at), (parts,), jnp.float32, low / len(pieces), high / len(pieces)))
        level = level * jnp.repeat(steps, extent[axis_at] // parts).reshape([-1 if axis == axis_at else 1 for axis in range(len(extent))])
    return level


def bell_draw(rng, shape, deviation, most, pieces=(), kind=jnp.bfloat16):
    loudness = block_levels(rng, shape, pieces, -0.22, 0.18) if pieces else 1.0
    values = jax.random.normal(rng, shape, jnp.float32) * deviation * loudness
    return jnp.minimum(jnp.maximum(values, -most), most).astype(kind)


def setup_inputs(seed: int = 0) -> dict:
    key_list = jax.random.split(jax.random.key(seed), 10)
    hidden_in = bell_draw(key_list[0], (TOKENS, D), 1.0, 6.0, ((0, 32),))
    segment_ids = draw_segment_ids(jax.random.fold_in(key_list[9], 71), 0)
    qkv_weight = draw_qkv_weight(jax.random.fold_in(key_list[9], 71), 0)
    out_weight = bell_draw(key_list[3], (HEADS * HD, D), (HEADS * HD // 16) ** -0.5, 0.875, ((0, 4),))
    norm1_gain = jnp.clip(1.0 + 0.18 * jax.random.normal(key_list[4], (D,), jnp.float32), 0.1, 1.9)
    in_weight = bell_draw(key_list[5], (D, 2, FF), D ** -0.5, 0.21875, ((2, 4),))
    down_weight = bell_draw(key_list[6], (FF, D), FF ** -0.5, 0.1875, ((0, 4),))
    norm2_gain = jnp.clip(1.0 + 0.18 * jax.random.normal(key_list[7], (D,), jnp.float32), 0.1, 1.9)
    cotangent = bell_draw(key_list[8], (TOKENS, D), 1.0, 6.0, ((0, 32),))
    return {"hidden_in": hidden_in, "segment_ids": segment_ids, "qkv_weight": qkv_weight, "out_weight": out_weight, "norm1_gain": norm1_gain, "in_weight": in_weight, "down_weight": down_weight, "norm2_gain": norm2_gain, "cotangent": cotangent}


rope_base = 160000.0
norm_eps = 1e-05
mask_fill = -1e+30

def token_positions(segments):
    length = segments.shape[0]
    places = jnp.arange(length, dtype=jnp.int32)
    before = jnp.concatenate([segments[:1] - 1, segments[:-1]])
    starts = lax.cummax(jnp.where(segments != before, places, 0), axis=0)
    return (places - starts).astype(jnp.float32)

def rope_tables(segments, head_size):
    half_size = head_size // 2
    freqs = rope_base ** (-(jnp.arange(half_size, dtype=jnp.float32) * 2.0 / head_size))
    angles = token_positions(segments)[:, None] * freqs[None, :]
    return (jnp.cos(angles)[:, None, :], jnp.sin(angles)[:, None, :])

def rotate(values, cosine, sine_part):
    half_size = values.shape[-1] // 2
    first, second = (values[..., :half_size], values[..., half_size:])
    return jnp.concatenate([first * cosine - second * sine_part, second * cosine + first * sine_part], -1)

def unrotate(grads, cosine, sine_part):
    half_size = grads.shape[-1] // 2
    first, second = (grads[..., :half_size], grads[..., half_size:])
    return jnp.concatenate([first * cosine + second * sine_part, second * cosine - first * sine_part], -1)

def norm_forward(values, gain):
    centred = values - lax.optimization_barrier(jnp.mean(values, -1, keepdims=True))
    scale_row = lax.rsqrt(lax.optimization_barrier(jnp.mean(centred * centred, -1, keepdims=True)) + norm_eps)
    normed = centred * scale_row
    return (normed * gain, normed, scale_row)

def norm_backward(grad_out, normed, scale_row, gain):
    scaled = grad_out * gain
    grad_values = scale_row * (scaled - lax.optimization_barrier(jnp.mean(scaled, -1, keepdims=True)) - normed * lax.optimization_barrier(jnp.mean(scaled * normed, -1, keepdims=True)))
    return (grad_values, lax.optimization_barrier(jnp.sum(grad_out * normed, 0)))

def scores_of(query, keys, segments):
    scores = jnp.einsum('thd,uhd->htu', query.astype(jnp.float32), keys.astype(jnp.float32)) / 8.0
    same = (segments[:, None] == segments[None, :])[None]
    return jnp.where(same, scores, mask_fill)

def attend(query, keys, values, segments):
    scores = scores_of(query, keys, segments)
    top = lax.optimization_barrier(jnp.max(scores, -1, keepdims=True))
    log_total = top + jnp.log(lax.optimization_barrier(jnp.sum(jnp.exp(scores - top), -1, keepdims=True)))
    probs = jnp.exp(scores - log_total).astype(jnp.bfloat16)
    attended = jnp.einsum('htu,uhd->thd', probs.astype(jnp.float32), values.astype(jnp.float32))
    return (attended.astype(jnp.bfloat16), log_total)

def attend_back(query, keys, values, segments, attended, log_total, grad_att):
    probs = jnp.exp(scores_of(query, keys, segments) - log_total)
    probs_low = probs.astype(jnp.bfloat16).astype(jnp.float32)
    grad_f = grad_att.astype(jnp.float32)
    grad_value = jnp.einsum('htu,thd->uhd', probs_low, grad_f)
    grad_probs = jnp.einsum('thd,uhd->htu', grad_f, values.astype(jnp.float32))
    delta = jnp.transpose(lax.optimization_barrier(jnp.sum(grad_f * attended.astype(jnp.float32), -1)))[:, :, None]
    grad_scores = (probs * (grad_probs - delta)).astype(jnp.bfloat16).astype(jnp.float32)
    grad_query = jnp.einsum('htu,uhd->thd', grad_scores, keys.astype(jnp.float32)) / 8.0
    grad_keys = jnp.einsum('htu,thd->uhd', grad_scores, query.astype(jnp.float32)) / 8.0
    return (grad_query, grad_keys, grad_value)

def gated(both):
    return jax.nn.gelu(both[:, 0], approximate=False) * both[:, 1]

def layer(inputs, segments, upstream, qkv_weight, out_weight, norm1_gain, in_weight, down_weight, norm2_gain):
    rows_all = inputs.shape[0]
    width = inputs.shape[1]
    heads_all = qkv_weight.shape[2] // HD
    hidden_all = in_weight.shape[2]
    qkv_flat = qkv_weight.reshape(width, -1)
    in_flat = in_weight.reshape(width, -1)
    cosine, sine_part = rope_tables(segments, HD)
    input_f = inputs.astype(jnp.float32)
    first_out, normed1, scale1 = norm_forward(input_f, norm1_gain)
    first_low = first_out.astype(jnp.bfloat16)
    projected = jnp.dot(first_low, qkv_flat, preferred_element_type=jnp.float32).reshape(rows_all, 3, heads_all, HD)
    query = rotate(projected[:, 0], cosine, sine_part).astype(jnp.bfloat16)
    keys = rotate(projected[:, 1], cosine, sine_part).astype(jnp.bfloat16)
    values = projected[:, 2].astype(jnp.bfloat16)
    attended, log_total = attend(query, keys, values, segments)
    att_flat = attended.reshape(rows_all, -1)
    resid = input_f + jnp.dot(att_flat, out_weight, preferred_element_type=jnp.float32)
    second_out, normed2, scale2 = norm_forward(resid, norm2_gain)
    second_low = second_out.astype(jnp.bfloat16)
    both = jnp.dot(second_low, in_flat, preferred_element_type=jnp.float32).reshape(rows_all, 2, hidden_all)
    active, gated_back = jax.vjp(gated, both)
    active_low = active.astype(jnp.bfloat16)
    output = resid + jnp.dot(active_low, down_weight, preferred_element_type=jnp.float32)
    grad_down = jnp.dot(active_low.T, upstream, preferred_element_type=jnp.float32)
    grad_active = jnp.dot(upstream, down_weight.T, preferred_element_type=jnp.float32)
    grad_both = gated_back(grad_active)[0].astype(jnp.bfloat16).reshape(rows_all, -1)
    grad_in = jnp.dot(second_low.T, grad_both, preferred_element_type=jnp.float32).reshape(in_weight.shape)
    grad_second = jnp.dot(grad_both, in_flat.T, preferred_element_type=jnp.float32)
    grad_resid, grad_norm2 = norm_backward(grad_second, normed2, scale2, norm2_gain)
    grad_resid = grad_resid + upstream.astype(jnp.float32)
    resid_low = grad_resid.astype(jnp.bfloat16)
    grad_out = jnp.dot(att_flat.T, resid_low, preferred_element_type=jnp.float32)
    grad_att = jnp.dot(resid_low, out_weight.T, preferred_element_type=jnp.float32).astype(jnp.bfloat16).reshape(rows_all, heads_all, HD)
    grad_query, grad_keys, grad_value = attend_back(query, keys, values, segments, attended, log_total, grad_att)
    grad_proj = jnp.stack([unrotate(grad_query, cosine, sine_part), unrotate(grad_keys, cosine, sine_part), grad_value], 1)
    grad_proj = grad_proj.astype(jnp.bfloat16).reshape(rows_all, -1)
    grad_qkv = jnp.dot(first_low.T, grad_proj, preferred_element_type=jnp.float32).reshape(qkv_weight.shape)
    grad_first = jnp.dot(grad_proj, qkv_flat.T, preferred_element_type=jnp.float32)
    grad_inputs, grad_norm1 = norm_backward(grad_first, normed1, scale1, norm1_gain)
    grad_inputs = grad_inputs + grad_resid
    return (output, grad_inputs, (grad_qkv, grad_out, grad_norm1, grad_in, grad_down, grad_norm2))

def reference(hidden_in, segment_ids, qkv_weight, out_weight, norm1_gain, in_weight, down_weight, norm2_gain, cotangent):
    blocks = TOKENS // TOK_DEV
    width = hidden_in.shape[1]
    inputs = hidden_in.reshape(blocks, TOK_DEV, width)
    segments = segment_ids.reshape(blocks, TOK_DEV)
    upstream = cotangent.reshape(blocks, TOK_DEV, width)
    zero_grads = (jnp.zeros(qkv_weight.shape, jnp.float32), jnp.zeros(out_weight.shape, jnp.float32), jnp.zeros(norm1_gain.shape, jnp.float32), jnp.zeros(in_weight.shape, jnp.float32), jnp.zeros(down_weight.shape, jnp.float32), jnp.zeros(norm2_gain.shape, jnp.float32))

    def one_block(totals, item):
        block_in, block_seg, block_up = item
        output, grad_inputs, grads = layer(block_in, block_seg, block_up, qkv_weight, out_weight, norm1_gain, in_weight, down_weight, norm2_gain)
        return (jax.tree.map(lambda left, right: left + right, totals, grads), (output, grad_inputs))
    totals, (outputs, grad_inputs) = lax.scan(one_block, zero_grads, (inputs, segments, upstream))
    grad_qkv, grad_out, grad_norm1, grad_in, grad_down, grad_norm2 = totals
    return (outputs.reshape(TOKENS, width), grad_inputs.reshape(TOKENS, width), grad_qkv, grad_out, grad_norm1, grad_in, grad_down, grad_norm2)
```

```python
import functools

import jax
import jax.numpy as jnp
from jax import lax
from jax.sharding import PartitionSpec as P

HD = 64


rope_base = 160000.0
norm_eps = 1e-05
mask_fill = -1e30


def token_positions(segments):
    length = segments.shape[0]
    places = jnp.arange(length, dtype=jnp.int32)
    before = jnp.concatenate([segments[:1] - 1, segments[:-1]])
    starts = lax.cummax(jnp.where(segments != before, places, 0), axis=0)
    return (places - starts).astype(jnp.float32)


def rope_tables(segments, head_size):
    half_size = head_size // 2
    freqs = rope_base ** (-(jnp.arange(half_size, dtype=jnp.float32) * 2.0 / head_size))
    angles = token_positions(segments)[:, None] * freqs[None, :]
    return (jnp.cos(angles)[:, None, :], jnp.sin(angles)[:, None, :])


def rotate(values, cosine, sine_part):
    half_size = values.shape[-1] // 2
    first, second = (values[..., :half_size], values[..., half_size:])
    return jnp.concatenate(
        [first * cosine - second * sine_part, second * cosine + first * sine_part], -1
    )


def unrotate(grads, cosine, sine_part):
    half_size = grads.shape[-1] // 2
    first, second = (grads[..., :half_size], grads[..., half_size:])
    return jnp.concatenate(
        [first * cosine + second * sine_part, second * cosine - first * sine_part], -1
    )


def norm_forward(values, gain):
    centred = values - jnp.mean(values, -1, keepdims=True)
    scale_row = lax.rsqrt(jnp.mean(centred * centred, -1, keepdims=True) + norm_eps)
    normed = centred * scale_row
    return (normed * gain, normed, scale_row)


def norm_backward(grad_out, normed, scale_row, gain):
    scaled = grad_out * gain
    grad_values = scale_row * (
        scaled
        - jnp.mean(scaled, -1, keepdims=True)
        - normed * jnp.mean(scaled * normed, -1, keepdims=True)
    )
    return (grad_values, jnp.sum(grad_out * normed, 0))


def scores_of(query, keys, segments):
    scores = jnp.einsum("thd,uhd->htu", query, keys, preferred_element_type=jnp.float32) / 8.0
    same = (segments[:, None] == segments[None, :])[None]
    return jnp.where(same, scores, mask_fill)


def attend(query, keys, values, segments):
    scores = scores_of(query, keys, segments)
    top = jnp.max(scores, -1, keepdims=True)
    log_total = top + jnp.log(jnp.sum(jnp.exp(scores - top), -1, keepdims=True))
    probs = jnp.exp(scores - log_total).astype(jnp.bfloat16)
    attended = jnp.einsum("htu,uhd->thd", probs, values, preferred_element_type=jnp.float32)
    return (attended.astype(jnp.bfloat16), log_total)


def attend_back(query, keys, values, segments, attended, log_total, grad_att):
    probs = jnp.exp(scores_of(query, keys, segments) - log_total)
    probs_low = probs.astype(jnp.bfloat16)
    grad_value = jnp.einsum("htu,thd->uhd", probs_low, grad_att, preferred_element_type=jnp.float32)
    grad_probs = jnp.einsum("thd,uhd->htu", grad_att, values, preferred_element_type=jnp.float32)
    delta = jnp.transpose(jnp.sum(grad_att.astype(jnp.float32) * attended.astype(jnp.float32), -1))[
        :, :, None
    ]
    grad_scores = (probs * (grad_probs - delta)).astype(jnp.bfloat16)
    grad_query = (
        jnp.einsum("htu,uhd->thd", grad_scores, keys, preferred_element_type=jnp.float32) / 8.0
    )
    grad_keys = (
        jnp.einsum("htu,thd->uhd", grad_scores, query, preferred_element_type=jnp.float32) / 8.0
    )
    return (grad_query, grad_keys, grad_value)


def gated(both):
    return jax.nn.gelu(both[:, 0], approximate=False) * both[:, 1]


def flip(value, axis_name, size, mask):
    return lax.ppermute(value, axis_name, [(at, at ^ mask) for at in range(size)])


def pick(value, place, axis):
    return lax.dynamic_index_in_dim(value, place, axis, keepdims=False)


def scatter_sum(pieces, axis_name, size):
    me = lax.axis_index(axis_name)
    mask = 1
    while mask < size:
        mine = (me // mask) % 2
        pairs = pieces.reshape((pieces.shape[0] // 2, 2) + pieces.shape[1:])
        outgoing = pick(pairs, 1 - mine, 1).astype(jnp.bfloat16)
        arrived = flip(outgoing, axis_name, size, mask)
        pieces = pick(pairs, mine, 1) + arrived.astype(jnp.float32)
        mask *= 2
    return pieces[0]


def gather_pieces(piece, axis_name, size):
    me = lax.axis_index(axis_name)
    pieces = piece[None]
    mask = size // 2
    while mask >= 1:
        mine = (me // mask) % 2
        arrived = flip(pieces, axis_name, size, mask)
        first = jnp.where(mine == 0, pieces, arrived)
        second = jnp.where(mine == 0, arrived, pieces)
        pieces = jnp.stack([first, second], 1).reshape((-1,) + piece.shape)
        mask //= 2
    return pieces


def dp_total(rows, size):
    count, width = rows.shape
    step = 8 * size
    padded = -(-count // step) * step
    rows = jnp.pad(rows, ((0, padded - count), (0, 0)))
    own = scatter_sum(rows.reshape(size, padded // size, width), "dp", size)
    full = gather_pieces(own.astype(jnp.bfloat16), "dp", size)
    return full.reshape(padded, width)[:count].astype(jnp.float32)


def gain_total(parts, dp, tensor):
    for axis_name, size in (("tensor", tensor), ("dp", dp)):
        mask = 1
        while mask < size:
            parts = parts + flip(parts, axis_name, size, mask)
            mask *= 2
    return parts


def body(
    hidden_in,
    segment_ids,
    qkv_weight,
    out_weight,
    norm1_gain,
    in_weight,
    down_weight,
    norm2_gain,
    cotangent,
    *,
    dp,
    tensor,
):
    width = hidden_in.shape[1]
    rows_here = hidden_in.shape[0]
    rows_all = segment_ids.shape[0]
    heads_here = qkv_weight.shape[2] // HD
    hidden_here = in_weight.shape[2]
    qkv_rows = jnp.transpose(qkv_weight, (1, 2, 0)).reshape(-1, width)
    in_rows = jnp.transpose(in_weight, (1, 2, 0)).reshape(-1, width)
    cosine, sine_part = rope_tables(segment_ids, HD)
    input_f = hidden_in.astype(jnp.float32)
    first_out, normed1, scale1 = norm_forward(input_f, norm1_gain)

    def tensor_sum(partial):
        return scatter_sum(partial.reshape(tensor, rows_here, width), "tensor", tensor)

    first_low, upstream = (
        lax.all_gather(first_out.astype(jnp.bfloat16), "tensor", axis=0, tiled=True),
        lax.all_gather(cotangent, "tensor", axis=0, tiled=True),
    )
    projected = jnp.einsum(
        "tw,fw->tf", first_low, qkv_rows, preferred_element_type=jnp.float32
    ).reshape(rows_all, 3, heads_here, HD)
    query = rotate(projected[:, 0], cosine, sine_part).astype(jnp.bfloat16)
    keys = rotate(projected[:, 1], cosine, sine_part).astype(jnp.bfloat16)
    values = projected[:, 2].astype(jnp.bfloat16)
    attended, log_total = attend(query, keys, values, segment_ids)
    att_flat = attended.reshape(rows_all, -1)
    resid = input_f + tensor_sum(jnp.dot(att_flat, out_weight, preferred_element_type=jnp.float32))
    second_out, normed2, scale2 = norm_forward(resid, norm2_gain)
    second_low = lax.all_gather(second_out.astype(jnp.bfloat16), "tensor", axis=0, tiled=True)
    both = jnp.einsum(
        "tw,fw->tf", second_low, in_rows, preferred_element_type=jnp.float32
    ).reshape(rows_all, 2, hidden_here)
    active, gated_back = jax.vjp(gated, both)
    active_low = active.astype(jnp.bfloat16)
    layer_out = resid + tensor_sum(
        jnp.dot(active_low, down_weight, preferred_element_type=jnp.float32)
    )
    grad_active = jnp.dot(upstream, down_weight.T, preferred_element_type=jnp.float32)
    grad_both = gated_back(grad_active)[0].astype(jnp.bfloat16).reshape(rows_all, -1)
    grad_second = tensor_sum(jnp.dot(grad_both, in_rows, preferred_element_type=jnp.float32))
    grad_in = jnp.dot(grad_both.T, second_low, preferred_element_type=jnp.float32)
    grad_down = jnp.dot(active_low.T, upstream, preferred_element_type=jnp.float32)
    early = dp_total(jnp.concatenate([grad_in, grad_down], 0), dp)
    grad_in = early[: 2 * hidden_here].reshape(2, hidden_here, width).transpose(2, 0, 1)
    grad_down = early[2 * hidden_here :]
    grad_resid, norm2_part = norm_backward(grad_second, normed2, scale2, norm2_gain)
    grad_resid = grad_resid + cotangent.astype(jnp.float32)
    resid_low = lax.all_gather(grad_resid.astype(jnp.bfloat16), "tensor", axis=0, tiled=True)
    grad_att = (
        jnp.dot(resid_low, out_weight.T, preferred_element_type=jnp.float32)
        .astype(jnp.bfloat16)
        .reshape(rows_all, heads_here, HD)
    )
    grad_query, grad_keys, grad_value = attend_back(
        query, keys, values, segment_ids, attended, log_total, grad_att
    )
    grad_proj = jnp.stack(
        [
            unrotate(grad_query, cosine, sine_part),
            unrotate(grad_keys, cosine, sine_part),
            grad_value,
        ],
        1,
    )
    grad_proj = grad_proj.astype(jnp.bfloat16).reshape(rows_all, -1)
    grad_first = tensor_sum(jnp.dot(grad_proj, qkv_rows, preferred_element_type=jnp.float32))
    grad_qkv = jnp.dot(grad_proj.T, first_low, preferred_element_type=jnp.float32)
    grad_out = jnp.dot(att_flat.T, resid_low, preferred_element_type=jnp.float32)
    late = dp_total(jnp.concatenate([grad_qkv, grad_out], 0), dp)
    grad_qkv = late[: 3 * heads_here * HD].reshape(3, heads_here * HD, width).transpose(2, 0, 1)
    grad_out = late[3 * heads_here * HD :]
    grad_inputs, norm1_part = norm_backward(grad_first, normed1, scale1, norm1_gain)
    grad_input = grad_inputs + grad_resid
    gains = gain_total(jnp.stack([norm1_part, norm2_part]), dp, tensor)
    return (
        layer_out,
        grad_input,
        grad_qkv,
        grad_out,
        gains[0],
        grad_in,
        grad_down,
        gains[1],
    )


def solution(mesh):
    in_specs = (
        P(("dp", "tensor"), None),
        P("dp"),
        P(None, None, "tensor"),
        P("tensor", None),
        P(),
        P(None, None, "tensor"),
        P("tensor", None),
        P(),
        P(("dp", "tensor"), None),
    )
    out_specs = (
        P(("dp", "tensor"), None),
        P(("dp", "tensor"), None),
        P(None, None, "tensor"),
        P("tensor", None),
        P(),
        P(None, None, "tensor"),
        P("tensor", None),
        P(),
    )
    dp, tensor = mesh.shape["dp"], mesh.shape["tensor"]
    run = functools.partial(body, dp=dp, tensor=tensor)
    return jax.shard_map(run, mesh=mesh, in_specs=in_specs, out_specs=out_specs, check_vma=False)
```

```python
import functools

import jax
import jax.numpy as jnp
from jax import lax
from jax.experimental import pallas as pl
from jax.experimental.pallas import tpu as pltpu
from jax.sharding import PartitionSpec as P

HD = 64
HALF = HD // 2
ROPE_BASE = 160000.0
EPS = 1e-05
FILL = -1e30
LOW = jnp.bfloat16
F32 = jnp.float32


def dot_nn(left, right):
    return lax.dot_general(left, right, (((1,), (0,)), ((), ())), preferred_element_type=F32)


def dot_nt(left, right):
    return lax.dot_general(left, right, (((1,), (1,)), ((), ())), preferred_element_type=F32)


def dot_tn(left, right):
    return lax.dot_general(left, right, (((0,), (0,)), ((), ())), preferred_element_type=F32)


def kernel_call(body, outs, *args, scratch=(), scalars=0, name=None):
    shapes = [jax.ShapeDtypeStruct(shape, kind) for shape, kind in outs]
    specs = [pl.BlockSpec(memory_space=pltpu.SMEM)] * scalars
    specs += [pl.BlockSpec(memory_space=pltpu.VMEM)] * (len(args) - scalars)
    return pl.pallas_call(
        body,
        out_shape=shapes,
        in_specs=specs,
        out_specs=[pl.BlockSpec(memory_space=pltpu.VMEM)] * len(shapes),
        scratch_shapes=list(scratch),
        name=name,
    )(*args)


def reversed_order(size):
    bits = size.bit_length() - 1
    return [int(format(at, f"0{bits}b")[::-1], 2) if bits else 0 for at in range(size)]


def flip(value, axis_name, size, mask):
    return lax.ppermute(value, axis_name, [(at, at ^ mask) for at in range(size)])


def gather_rows(piece, size):
    have = {0: piece}
    mask = size // 2
    while mask >= 1:
        for at in sorted(have):
            have[at | mask] = flip(have[at], "tensor", size, mask)
        mask //= 2
    return [have[at] for at in reversed_order(size)]


def token_positions(segments):
    length = segments.shape[0]
    places = jnp.arange(length, dtype=jnp.int32)
    before = jnp.concatenate([segments[:1] - 1, segments[:-1]])
    starts = lax.cummax(jnp.where(segments != before, places, 0), axis=0)
    return (places - starts).astype(F32)


def norm_rows(values, gain):
    centred = values - jnp.mean(values, -1, keepdims=True)
    scale_row = lax.rsqrt(jnp.mean(centred * centred, -1, keepdims=True) + EPS)
    normed = centred * scale_row
    return normed * gain, normed, scale_row


def norm_back(grad_out, normed, scale_row, gain):
    scaled = grad_out * gain
    grad_values = scale_row * (
        scaled
        - jnp.mean(scaled, -1, keepdims=True)
        - normed * jnp.mean(scaled * normed, -1, keepdims=True)
    )
    return grad_values, jnp.sum(grad_out * normed, 0, keepdims=True)


def split_partial(partial, keep_ref, send_ref):
    half = partial.shape[0] // 2
    keep_ref[...] = partial[:half]
    send_ref[...] = partial[half:].astype(LOW)


def attend_kernel(*refs, pieces):
    parts = refs[:pieces]
    (gain, wqkv, wout, cosine, sine, seg, qkv_ref, p_ref, o_ref, h_ref, keep, send) = refs[pieces:]
    rows = jnp.concatenate([part[...] for part in parts], 0).astype(F32)
    first = norm_rows(rows, gain[...])[0].astype(LOW)
    h_ref[...] = first
    proj = dot_nt(wqkv[...], first)
    heads = wout.shape[0] // HD
    cos, sin = cosine[...], sine[...]
    made = []
    for at in range(2 * heads):
        upper = proj[at * HD : at * HD + HALF]
        lower = proj[at * HD + HALF : (at + 1) * HD]
        made += [upper * cos - lower * sin, lower * cos + upper * sin]
    made.append(proj[2 * heads * HD :])
    qkv_ref[...] = jnp.concatenate(made, 0).astype(LOW)
    count = seg.shape[1]
    row = seg[...]
    column = jnp.transpose(jnp.broadcast_to(row, (128, count)))[:, :1]
    same = column == row
    for head in range(heads):
        query = qkv_ref[head * HD : (head + 1) * HD, :]
        keys = qkv_ref[(heads + head) * HD : (heads + head + 1) * HD, :]
        values = qkv_ref[(2 * heads + head) * HD : (2 * heads + head + 1) * HD, :]
        scores = jnp.where(same, dot_tn(keys, query) * 0.125, FILL)
        top = jnp.max(scores, 0, keepdims=True)
        raised = jnp.exp(scores - top)
        total = jnp.sum(raised, 0, keepdims=True)
        probs = (raised * (1.0 / total)).astype(LOW)
        p_ref[head] = probs
        o_ref[head * HD : (head + 1) * HD, :] = dot_nn(values, probs).astype(LOW)
    split_partial(dot_tn(o_ref[...], wout[...]), keep, send)


def fold_kernel(keep, came, own_ref, send_ref):
    half = own_ref.shape[0]
    total = keep[...] + came[...].astype(F32)
    own_ref[...] = total[:half]
    send_ref[...] = total[half:].astype(LOW)


def second_norm_kernel(hidden, own, came, gain, resid_ref, low_ref):
    resid = hidden[...].astype(F32) + own[...] + came[...].astype(F32)
    resid_ref[...] = resid
    low_ref[...] = norm_rows(resid, gain[...])[0].astype(LOW)


def grad_active_kernel(*refs, pieces):
    down, da_ref, up_ref = refs[pieces:]
    rows = jnp.concatenate([part[...] for part in refs[:pieces]], 0)
    up_ref[...] = rows
    da_ref[...] = dot_nt(down[...], rows)


def forward_back_kernel(*refs, pieces):
    in_rows, grad_active, low_ref, active_ref, both_ref, keep, send = refs[pieces:]
    rows = jnp.concatenate([part[...] for part in refs[:pieces]], 0)
    low_ref[...] = rows
    both = dot_nt(in_rows[...], rows)
    hidden = both.shape[0] // 2
    gate, up = both[:hidden], both[hidden:]
    below = 0.5 * (1.0 + lax.erf(gate * (0.5**0.5)))
    bell = jnp.exp(-0.5 * gate * gate) * 0.3989422804014327
    active = gate * below
    active_ref[...] = (active * up).astype(LOW)
    came = grad_active[...]
    both_ref[:hidden, :] = (came * up * (below + gate * bell)).astype(LOW)
    both_ref[hidden:, :] = (came * active).astype(LOW)
    split_partial(dot_tn(both_ref[...], in_rows[...]), keep, send)


def down_kernel(active, down, keep, send):
    split_partial(dot_tn(active[...], down[...]), keep, send)


def emit_chunks(place, total, keep, send, size):
    step = total.shape[0] // size
    order = reversed_order(size)
    half = size // 2

    def chunk(offset):
        start = pl.multiple_of((place ^ offset) * step, 8)
        return total[pl.ds(start, step), :]

    keep[...] = jnp.concatenate([chunk(at) for at in order[:half]], 0)
    send[...] = jnp.concatenate([chunk(at) for at in order[half:]], 0).astype(LOW)


def two_grads_kernel(place, left_a, right_a, left_b, right_b, keep, send, total, *, size):
    rows_a, rows_b = left_a.shape[0], left_b.shape[0]
    total[:rows_a, :] = dot_nn(left_a[...], right_a[...])
    total[rows_a : rows_a + rows_b, :] = dot_nn(left_b[...], right_b[...])
    if total.shape[0] > rows_a + rows_b:
        total[rows_a + rows_b :, :] = jnp.zeros(
            (total.shape[0] - rows_a - rows_b, total.shape[1]), F32
        )
    emit_chunks(place[0], total, keep, send, size)


def low_kernel(keep, came, out_ref):
    out_ref[...] = (keep[...] + came[...].astype(F32)).astype(LOW)


def join_kernel(first, second, out_ref):
    out_ref[...] = jnp.concatenate([first[...].astype(F32), second[...].astype(F32)], 0).astype(LOW)


def place_kernel(place, first, second, out_a, out_b, total, *, size):
    step = total.shape[0] // size
    order = reversed_order(size)
    half = size // 2
    both = (first[...].astype(F32), second[...].astype(F32))
    for at, offset in enumerate(order):
        rows = both[at // half][(at % half) * step : (at % half + 1) * step]
        total[pl.ds(pl.multiple_of((place[0] ^ offset) * step, 8), step), :] = rows
    out_a[...] = total[: out_a.shape[0], :]
    out_b[...] = total[out_a.shape[0] : out_a.shape[0] + out_b.shape[0], :]


def resid_grad_kernel(own, came, resid, gain, up, grad_ref, low_ref, gain_ref):
    _, normed, scale_row = norm_rows(resid[...], gain[...])
    grad_second = own[...] + came[...].astype(F32)
    grad, gain_ref[...] = norm_back(grad_second, normed, scale_row, gain[...])
    grad = grad + up[...].astype(F32)
    grad_ref[...] = grad
    low_ref[...] = grad.astype(LOW)


def attend_back_kernel(*refs, pieces):
    (wout, wqkv, qkv, probs, attended, cosine, sine, low_ref, dqkv_ref, keep, send) = refs[pieces:]
    rows = jnp.concatenate([part[...] for part in refs[:pieces]], 0)
    low_ref[...] = rows
    heads = wout.shape[0] // HD
    grad_att = dot_nt(wout[...], rows).astype(LOW)
    cos, sin = cosine[...], sine[...]
    made = [None] * (3 * heads)

    def turned_back(grad):
        upper, lower = grad[:HALF], grad[HALF:]
        return jnp.concatenate([upper * cos + lower * sin, lower * cos - upper * sin], 0)

    for head in range(heads):
        span = slice(head * HD, (head + 1) * HD)
        grad = grad_att[span]
        query = qkv[head * HD : (head + 1) * HD, :]
        keys = qkv[(heads + head) * HD : (heads + head + 1) * HD, :]
        values = qkv[(2 * heads + head) * HD : (2 * heads + head + 1) * HD, :]
        delta = jnp.sum(grad.astype(F32) * attended[span, :].astype(F32), 0, keepdims=True)
        low = probs[head]
        grad_probs = dot_tn(values, grad)
        grad_scores = (low.astype(F32) * (grad_probs - delta)).astype(LOW)
        made[head] = turned_back(dot_nn(keys, grad_scores) * 0.125)
        made[heads + head] = turned_back(dot_nt(query, grad_scores) * 0.125)
        made[2 * heads + head] = dot_nt(grad, low)
    dqkv_ref[...] = jnp.concatenate(made, 0).astype(LOW)
    split_partial(dot_tn(dqkv_ref[...], wqkv[...]), keep, send)


def input_grad_kernel(own, came, hidden, gain, resid_grad, grad_ref, gain_ref):
    _, normed, scale_row = norm_rows(hidden[...].astype(F32), gain[...])
    grad_first = own[...] + came[...].astype(F32)
    grad, gain_ref[...] = norm_back(grad_first, normed, scale_row, gain[...])
    grad_ref[...] = grad + resid_grad[...]


def add_kernel(resid, own, came, out_ref):
    out_ref[...] = resid[...] + own[...] + came[...].astype(F32)


def body(
    hidden_in,
    segment_ids,
    qkv_weight,
    out_weight,
    norm1_gain,
    in_weight,
    down_weight,
    norm2_gain,
    cotangent,
    *,
    dp,
    tensor,
):
    width = hidden_in.shape[1]
    rows_here = hidden_in.shape[0]
    rows_all = segment_ids.shape[0]
    feats = out_weight.shape[0]
    heads = feats // HD
    units = down_weight.shape[0]
    half = rows_all // 2
    qkv_rows = jnp.transpose(qkv_weight, (1, 2, 0)).reshape(3 * feats, width)
    in_rows = jnp.transpose(in_weight, (1, 2, 0)).reshape(2 * units, width)
    gain1, gain2 = norm1_gain.reshape(1, width), norm2_gain.reshape(1, width)
    my_tensor = lax.axis_index("tensor")
    place = lax.axis_index("dp").astype(jnp.int32).reshape(1)
    order = reversed_order(tensor)

    def reorder(values):
        return jnp.concatenate(
            [
                lax.dynamic_slice_in_dim(values, (my_tensor ^ at) * rows_here, rows_here, -1)
                for at in order
            ],
            -1,
        )

    positions = reorder(token_positions(segment_ids))
    segments = reorder(segment_ids.astype(F32)).reshape(1, rows_all)
    freqs = ROPE_BASE ** (-(jnp.arange(HALF, dtype=F32) * 2.0 / HD))
    angles = freqs[:, None] * positions[None, :]
    cosine, sine = jnp.cos(angles), jnp.sin(angles)

    def scattered(keep, send):
        mask = 1
        while True:
            came = flip(send, "tensor", tensor, mask)
            mask *= 2
            if mask >= tensor:
                return keep, came
            rows = keep.shape[0] // 2
            keep, send = kernel_call(
                fold_kernel, [((rows, width), F32), ((rows, width), LOW)], keep, came
            )

    def dp_total(keep, send, count_a, count_b, padded):
        mask = 1
        while True:
            came = flip(send, "dp", dp, mask)
            mask *= 2
            if mask >= dp:
                break
            rows = keep.shape[0] // 2
            keep, send = kernel_call(
                fold_kernel, [((rows, width), F32), ((rows, width), LOW)], keep, came
            )
        own = kernel_call(low_kernel, [(keep.shape, LOW)], keep, came)[0]
        mask //= 2
        while True:
            came = flip(own, "dp", dp, mask)
            mask //= 2
            if mask < 1:
                break
            own = kernel_call(join_kernel, [((2 * own.shape[0], width), LOW)], own, came)[0]
        return kernel_call(
            functools.partial(place_kernel, size=dp),
            [((count_a, width), F32), ((count_b, width), F32)],
            place,
            own,
            came,
            scratch=[pltpu.VMEM((padded, width), F32)],
            scalars=1,
        )

    def two_grads(left_a, right_a, left_b, right_b):
        count_a, count_b = left_a.shape[0], left_b.shape[0]
        step = 8 * dp
        padded = -(-(count_a + count_b) // step) * step
        keep, send = kernel_call(
            functools.partial(two_grads_kernel, size=dp),
            [((padded // 2, width), F32), ((padded // 2, width), LOW)],
            place,
            left_a,
            right_a,
            left_b,
            right_b,
            scratch=[pltpu.VMEM((padded, width), F32)],
            scalars=1,
            name="two_grads",
        )
        return dp_total(keep, send, count_a, count_b, padded)

    hidden_parts = gather_rows(hidden_in, tensor)
    up_parts = gather_rows(cotangent, tensor)
    halves = [((half, width), F32), ((half, width), LOW)]
    qkv, probs, attended, first_low, keep, send = kernel_call(
        functools.partial(attend_kernel, pieces=tensor),
        [
            ((3 * feats, rows_all), LOW),
            ((heads, rows_all, rows_all), LOW),
            ((feats, rows_all), LOW),
            ((rows_all, width), LOW),
        ]
        + halves,
        *hidden_parts,
        gain1,
        qkv_rows,
        out_weight,
        cosine,
        sine,
        segments,
        name="attend",
    )
    own, came = scattered(keep, send)
    resid, second_own = kernel_call(
        second_norm_kernel,
        [((rows_here, width), F32), ((rows_here, width), LOW)],
        hidden_in,
        own,
        came,
        gain2,
        name="second_norm",
    )
    grad_active, upstream = kernel_call(
        functools.partial(grad_active_kernel, pieces=tensor),
        [((units, rows_all), F32), ((rows_all, width), LOW)],
        *up_parts,
        down_weight,
        name="grad_active",
    )
    second_parts = gather_rows(second_own, tensor)
    second_low, active, grad_both, keep, send = kernel_call(
        functools.partial(forward_back_kernel, pieces=tensor),
        [((rows_all, width), LOW), ((units, rows_all), LOW), ((2 * units, rows_all), LOW)] + halves,
        *second_parts,
        in_rows,
        grad_active,
        name="forward_back",
    )
    own, came = scattered(keep, send)
    grad_resid, resid_own, norm2_part = kernel_call(
        resid_grad_kernel,
        [((rows_here, width), F32), ((rows_here, width), LOW), ((1, width), F32)],
        own,
        came,
        resid,
        gain2,
        cotangent,
        name="resid_grad",
    )
    resid_parts = gather_rows(resid_own, tensor)
    out_own, out_came = scattered(*kernel_call(down_kernel, halves, active, down_weight, name="down"))
    layer_out = kernel_call(
        add_kernel, [((rows_here, width), F32)], resid, out_own, out_came, name="layer_out"
    )[0]
    grad_in, grad_down = two_grads(grad_both, second_low, active, upstream)
    resid_low, grad_proj, keep, send = kernel_call(
        functools.partial(attend_back_kernel, pieces=tensor),
        [((rows_all, width), LOW), ((3 * feats, rows_all), LOW)] + halves,
        *resid_parts,
        out_weight,
        qkv_rows,
        qkv,
        probs,
        attended,
        cosine,
        sine,
        name="attend_back",
    )
    own, came = scattered(keep, send)
    grad_qkv, grad_out = two_grads(grad_proj, first_low, attended, resid_low)
    grad_input, norm1_part = kernel_call(
        input_grad_kernel,
        [((rows_here, width), F32), ((1, width), F32)],
        own,
        came,
        hidden_in,
        gain1,
        grad_resid,
        name="input_grad",
    )
    gains = jnp.concatenate([norm1_part, norm2_part], 0)
    for axis_name, size in (("tensor", tensor), ("dp", dp)):
        mask = 1
        while mask < size:
            gains = gains + flip(gains, axis_name, size, mask)
            mask *= 2
    return (
        layer_out,
        grad_input,
        grad_qkv.reshape(3, feats, width).transpose(2, 0, 1),
        grad_out,
        gains[0],
        grad_in.reshape(2, units, width).transpose(2, 0, 1),
        grad_down,
        gains[1],
    )


def solution(mesh):
    in_specs = (
        P(("dp", "tensor"), None),
        P("dp"),
        P(None, None, "tensor"),
        P("tensor", None),
        P(),
        P(None, None, "tensor"),
        P("tensor", None),
        P(),
        P(("dp", "tensor"), None),
    )
    out_specs = (
        P(("dp", "tensor"), None),
        P(("dp", "tensor"), None),
        P(None, None, "tensor"),
        P("tensor", None),
        P(),
        P(None, None, "tensor"),
        P("tensor", None),
        P(),
    )
    run = functools.partial(body, dp=mesh.shape["dp"], tensor=mesh.shape["tensor"])
    return jax.shard_map(run, mesh=mesh, in_specs=in_specs, out_specs=out_specs, check_vma=False)
```

```python
import functools

import jax
import jax.numpy as jnp
from jax import lax
from jax.experimental import pallas as pl
from jax.experimental.pallas import tpu as pltpu
from jax.sharding import PartitionSpec as P


HD = 64
HALF = HD // 2
ROPE_BASE = 160000.0
EPS = 1e-05
FILL = -1e30
LOW = jnp.bfloat16
F32 = jnp.float32


def dot_nn(left, right):
    return lax.dot_general(left, right, (((1,), (0,)), ((), ())), preferred_element_type=F32)


def dot_nt(left, right):
    return lax.dot_general(left, right, (((1,), (1,)), ((), ())), preferred_element_type=F32)


def dot_tn(left, right):
    return lax.dot_general(left, right, (((0,), (0,)), ((), ())), preferred_element_type=F32)


def kernel_call(body, outs, *args, scratch=(), scalars=0, room=6, scalar_out=False):
    shapes = [jax.ShapeDtypeStruct(shape, kind) for shape, kind in outs]
    specs = [pl.BlockSpec(memory_space=pltpu.SMEM)] * scalars
    specs += [pl.BlockSpec(memory_space=pltpu.VMEM)] * (len(args) - scalars)
    out_specs = [pl.BlockSpec(memory_space=pltpu.VMEM)] * len(shapes)
    if scalar_out:
        out_specs[-1] = pl.BlockSpec(memory_space=pltpu.SMEM)
    return pl.pallas_call(
        body,
        out_shape=shapes,
        in_specs=specs,
        out_specs=out_specs,
        scratch_shapes=list(scratch),
        compiler_params=pltpu.CompilerParams(vmem_limit_bytes=room << 20),
    )(*args)


def offsets_of(bits):
    made = [0]
    for bit in reversed(bits):
        made = made + [at | bit for at in made]
    return made


def bits_of(size):
    return tuple(1 << at for at in range(size.bit_length() - 1))


def flip(value, axis_name, size, mask):
    return lax.ppermute(value, axis_name, [(at, at ^ mask) for at in range(size)])


def gather_rows(piece, size):
    have = {0: piece}
    for bit in reversed(bits_of(size)):
        for at in sorted(have):
            have[at | bit] = flip(have[at], "tensor", size, bit)
    return [have[at] for at in offsets_of(bits_of(size))]


def tables_kernel(spot, seg, freqs, cos_ref, sin_ref, seg_ref, place_ref, rows, *, offsets):
    place_ref[0] = spot[1]
    ids = seg[...]
    count = ids.shape[1]
    lanes = lax.broadcasted_iota(jnp.int32, ids.shape, 1)
    before = jnp.where(lanes == 0, -1, pltpu.roll(ids, 1, 1))
    starts = jnp.where(ids != before, lanes, 0)
    reach = 1
    while reach < count:
        starts = jnp.maximum(starts, jnp.where(lanes >= reach, pltpu.roll(starts, reach, 1), 0))
        reach *= 2
    rows[0:1, :] = (lanes - starts).astype(F32)[0:1]
    rows[1:2, :] = ids.astype(F32)[0:1]
    step = count // len(offsets)
    turned = jnp.concatenate(
        [rows[:, pl.ds(pl.multiple_of((spot[0] ^ at) * step, step), step)] for at in offsets], 1
    )
    angles = freqs[...] * turned[0:1]
    cos_ref[...] = jnp.cos(angles)
    sin_ref[...] = jnp.sin(angles)
    seg_ref[...] = turned[1:2]


def norm_rows(values, gain):
    centred = values - jnp.mean(values, -1, keepdims=True)
    scale_row = lax.rsqrt(jnp.mean(centred * centred, -1, keepdims=True) + EPS)
    normed = centred * scale_row
    return normed * gain, normed, scale_row


def norm_back(grad_out, normed, scale_row, gain):
    scaled = grad_out * gain
    return scale_row * (
        scaled
        - jnp.mean(scaled, -1, keepdims=True)
        - normed * jnp.mean(scaled * normed, -1, keepdims=True)
    )


def split_partial(partial, keep_ref, send_ref):
    half = partial.shape[0] // 2
    keep_ref[...] = partial[:half]
    send_ref[...] = partial[half:].astype(LOW)


def attend_kernel(*refs, pieces):
    parts = refs[:pieces]
    (gain, wqkv, wout, cosine, sine, seg, qkv_ref, p_ref, o_ref, h_ref, keep, send) = refs[pieces:]
    rows = jnp.concatenate([part[...] for part in parts], 0).astype(F32)
    first = norm_rows(rows, gain[...])[0].astype(LOW)
    h_ref[...] = first
    proj = dot_nt(wqkv[...], first)
    heads = wout.shape[0] // HD
    cos, sin = cosine[...], sine[...]
    made = []
    for at in range(2 * heads):
        upper = proj[at * HD : at * HD + HALF]
        lower = proj[at * HD + HALF : (at + 1) * HD]
        made += [upper * cos - lower * sin, lower * cos + upper * sin]
    made.append(proj[2 * heads * HD :])
    qkv_ref[...] = jnp.concatenate(made, 0).astype(LOW)
    count = seg.shape[1]
    row = seg[...]
    column = jnp.transpose(jnp.broadcast_to(row, (128, count)))[:, :1]
    same = column == row
    for head in range(heads):
        query = qkv_ref[head * HD : (head + 1) * HD, :]
        keys = qkv_ref[(heads + head) * HD : (heads + head + 1) * HD, :]
        values = qkv_ref[(2 * heads + head) * HD : (2 * heads + head + 1) * HD, :]
        scores = jnp.where(same, dot_tn(keys, query) * 0.125, FILL)
        top = jnp.max(scores, 0, keepdims=True)
        raised = jnp.exp(scores - top)
        total = jnp.sum(raised, 0, keepdims=True)
        probs = (raised * (1.0 / total)).astype(LOW)
        p_ref[head] = probs
        o_ref[head * HD : (head + 1) * HD, :] = dot_nn(values, probs).astype(LOW)
    split_partial(dot_tn(o_ref[...], wout[...]), keep, send)


def fold_kernel(keep, came, own_ref, send_ref):
    half = own_ref.shape[0]
    total = keep[...] + came[...].astype(F32)
    own_ref[...] = total[:half]
    send_ref[...] = total[half:].astype(LOW)


def whole_fold_kernel(keep, came, own_ref, send_ref):
    total = keep[...] + came[...].astype(F32)
    own_ref[...] = total
    send_ref[...] = total.astype(LOW)


def swapped(came):
    half = came.shape[0] // 2
    return jnp.concatenate([came[half:], came[:half]], 0).astype(F32)


def second_norm_kernel(*refs):
    own, came, gain, resid_ref, low_ref = refs[-5:]
    hidden = jnp.concatenate([part[...] for part in refs[:-5]], 0).astype(F32)
    resid = hidden + own[...] + swapped(came[...])
    resid_ref[...] = resid
    low_ref[...] = norm_rows(resid, gain[...])[0].astype(LOW)


def grad_active_kernel(*refs, pieces):
    down, da_ref, up_ref = refs[pieces:]
    rows = jnp.concatenate([part[...] for part in refs[:pieces]], 0)
    up_ref[...] = rows
    da_ref[...] = dot_nt(down[...], rows)


def forward_back_kernel(*refs, pieces):
    in_rows, grad_active, low_ref, active_ref, both_ref, keep, send = refs[pieces:]
    rows = jnp.concatenate([part[...] for part in refs[:pieces]], 0)
    low_ref[...] = rows
    both = dot_nt(in_rows[...], rows)
    hidden = both.shape[0] // 2
    gate, up = both[:hidden], both[hidden:]
    below = 0.5 * (1.0 + lax.erf(gate * (0.5**0.5)))
    bell = jnp.exp(-0.5 * gate * gate) * 0.3989422804014327
    active = gate * below
    active_ref[...] = (active * up).astype(LOW)
    came = grad_active[...]
    both_ref[:hidden, :] = (came * up * (below + gate * bell)).astype(LOW)
    both_ref[hidden:, :] = (came * active).astype(LOW)
    split_partial(dot_tn(both_ref[...], in_rows[...]), keep, send)


def down_kernel(active, down, keep, send):
    split_partial(dot_tn(active[...], down[...]), keep, send)


def emit_chunks(place, total, first, rows, keep, send, bits):
    offsets = offsets_of(bits)
    step = rows // len(offsets)
    half = len(offsets) // 2

    def chunk(offset):
        return total[pl.ds(pl.multiple_of(first + (place ^ offset) * step, 8), step), :]

    keep[...] = jnp.concatenate([chunk(at) for at in offsets[:half]], 0)
    send[...] = jnp.concatenate([chunk(at) for at in offsets[half:]], 0).astype(LOW)


def two_grads_kernel(place, left_a, right_a, left_b, right_b, *refs, streams):
    total = refs[-1]
    rows_a, rows_b = left_a.shape[0], left_b.shape[0]
    total[:rows_a, :] = dot_nn(left_a[...], right_a[...])
    total[rows_a : rows_a + rows_b, :] = dot_nn(left_b[...], right_b[...])
    spare = total.shape[0] - rows_a - rows_b
    if spare:
        total[rows_a + rows_b :, :] = jnp.zeros((spare, total.shape[1]), F32)
    first = 0
    for at, (rows, bits) in enumerate(streams):
        emit_chunks(place[0], total, first, rows, refs[2 * at], refs[2 * at + 1], bits)
        first += rows


def two_lows(values):
    high = values.astype(LOW).astype(F32)
    return jnp.concatenate([high, values - high, jnp.zeros((12, values.shape[1]), F32)], 0)


def gains_from(rows):
    return rows[0:2] + rows[2:4]


def exchange_fold_kernel(keep, came, *refs):
    total = keep[...] + came[...].astype(F32)
    if len(refs) == 2:
        total = jnp.concatenate([total, two_lows(refs[0][...])], 0)
    refs[-1][...] = total.astype(LOW)


def add_pair_kernel(mine, came, out_ref, *, extra):
    ours, theirs = mine[...].astype(F32), came[...].astype(F32)
    rows = ours.shape[0] - extra
    total = ours[:rows] + swapped(theirs[:rows])
    if extra:
        gains = gains_from(ours[rows:]) + gains_from(theirs[rows:])
        total = jnp.concatenate([total, two_lows(gains)], 0)
    out_ref[...] = total.astype(LOW)


def join_kernel(mine, came, out_ref, *, extra):
    ours, theirs = mine[...].astype(F32), came[...].astype(F32)
    rows = ours.shape[0] - extra
    parts = [ours[:rows], theirs[:rows]]
    if extra:
        parts.append(two_lows(gains_from(ours[rows:]) + gains_from(theirs[rows:])))
    out_ref[...] = jnp.concatenate(parts, 0).astype(LOW)


def place_kernel(place, *refs, streams, extra):
    inputs, outs, total = refs[: 2 * len(streams)], refs[2 * len(streams) : -1], refs[-1]
    first = 0
    for at, (rows, bits) in enumerate(streams):
        ours = inputs[2 * at][...].astype(F32)
        theirs = inputs[2 * at + 1][...].astype(F32)
        offsets = offsets_of(bits)
        step = rows // len(offsets)
        half = rows // 2
        for spot, offset in enumerate(offsets):
            source, begin = (ours, spot * step) if spot * step < half else (theirs, spot * step - half)
            start = pl.multiple_of(first + (place[0] ^ offset) * step, 8)
            total[pl.ds(start, step), :] = source[begin : begin + step]
        if extra and at == len(streams) - 1:
            gains = gains_from(ours[half:]) + gains_from(theirs[half:])
            outs[2][...] = gains
        first += rows
    rows_a, rows_b = outs[0].shape[0], outs[1].shape[0]
    outs[0][...] = total[:rows_a, :]
    outs[1][...] = total[rows_a : rows_a + rows_b, :]


def resid_grad_kernel(*refs):
    own, came, resid, gain, grad_ref, low_ref, gain_ref = refs[-7:]
    up = jnp.concatenate([part[...] for part in refs[:-7]], 0).astype(F32)
    _, normed, scale_row = norm_rows(resid[...], gain[...])
    grad_second = own[...] + swapped(came[...])
    grad = norm_back(grad_second, normed, scale_row, gain[...]) + up
    rows = grad_ref.shape[0]
    grad_ref[...] = grad[:rows]
    low_ref[...] = grad.astype(LOW)
    gain_ref[...] = jnp.sum(grad_second[:rows] * normed[:rows], 0, keepdims=True)


def attend_back_kernel(*refs, pieces):
    (wout, wqkv, qkv, probs, attended, cosine, sine, low_ref, dqkv_ref, keep, send) = refs[pieces:]
    rows = jnp.concatenate([part[...] for part in refs[:pieces]], 0)
    low_ref[...] = rows
    heads = wout.shape[0] // HD
    grad_att = dot_nt(wout[...], rows).astype(LOW)
    cos, sin = cosine[...], sine[...]
    made = [None] * (3 * heads)

    def turned_back(grad):
        upper, lower = grad[:HALF], grad[HALF:]
        return jnp.concatenate([upper * cos + lower * sin, lower * cos - upper * sin], 0)

    for head in range(heads):
        span = slice(head * HD, (head + 1) * HD)
        grad = grad_att[span]
        query = qkv[head * HD : (head + 1) * HD, :]
        keys = qkv[(heads + head) * HD : (heads + head + 1) * HD, :]
        values = qkv[(2 * heads + head) * HD : (2 * heads + head + 1) * HD, :]
        delta = jnp.sum(grad.astype(F32) * attended[span, :].astype(F32), 0, keepdims=True)
        low = probs[head]
        grad_probs = dot_tn(values, grad)
        grad_scores = (low.astype(F32) * (grad_probs - delta)).astype(LOW)
        made[head] = turned_back(dot_nn(keys, grad_scores) * 0.125)
        made[heads + head] = turned_back(dot_nt(query, grad_scores) * 0.125)
        made[2 * heads + head] = dot_nt(grad, low)
    dqkv_ref[...] = jnp.concatenate(made, 0).astype(LOW)
    split_partial(dot_tn(dqkv_ref[...], wqkv[...]), keep, send)


def input_grad_kernel(own, came, hidden, gain, resid_grad, gain2_part, grad_ref, gain_ref):
    _, normed, scale_row = norm_rows(hidden[...].astype(F32), gain[...])
    grad_first = own[...] + came[...].astype(F32)
    grad_ref[...] = norm_back(grad_first, normed, scale_row, gain[...]) + resid_grad[...]
    gain_ref[0:1, :] = jnp.sum(grad_first * normed, 0, keepdims=True)
    gain_ref[1:2, :] = gain2_part[...]


def add_kernel(resid, own, came, out_ref):
    out_ref[...] = resid[: out_ref.shape[0], :] + own[...] + came[...].astype(F32)


def sum_kernel(mine, came, out_ref):
    out_ref[...] = mine[...] + came[...]


def early_orders(bits):
    return (bits,)


def late_orders(bits):
    return (bits,)


def body(
    hidden_in,
    segment_ids,
    qkv_weight,
    out_weight,
    norm1_gain,
    in_weight,
    down_weight,
    norm2_gain,
    cotangent,
    *,
    dp,
    tensor,
):
    width = hidden_in.shape[1]
    rows_here = hidden_in.shape[0]
    rows_all = segment_ids.shape[0]
    feats = out_weight.shape[0]
    heads = feats // HD
    units = down_weight.shape[0]
    half = rows_all // 2
    qkv_rows = jnp.transpose(qkv_weight, (1, 2, 0)).reshape(3 * feats, width)
    in_rows = jnp.transpose(in_weight, (1, 2, 0)).reshape(2 * units, width)
    gain1, gain2 = norm1_gain.reshape(1, width), norm2_gain.reshape(1, width)
    spot = jnp.stack([lax.axis_index("tensor"), lax.axis_index("dp")]).astype(jnp.int32)
    bits = bits_of(tensor)
    offsets = offsets_of(bits)
    freqs = (ROPE_BASE ** (-(jnp.arange(HALF, dtype=F32) * 2.0 / HD))).reshape(HALF, 1)
    hidden_parts = gather_rows(hidden_in, tensor)
    cosine, sine, segments, place = kernel_call(
        functools.partial(tables_kernel, offsets=offsets),
        [((HALF, rows_all), F32), ((HALF, rows_all), F32), ((1, rows_all), F32), ((1,), jnp.int32)],
        spot,
        segment_ids.reshape(1, rows_all),
        freqs,
        scratch=[pltpu.VMEM((2, rows_all), F32)],
        scalars=1,
        scalar_out=True,
    )
    up_parts = gather_rows(cotangent, tensor)

    def fold(keep, came):
        rows = keep.shape[0] // 2
        return kernel_call(fold_kernel, [((rows, width), F32), ((rows, width), LOW)], keep, came)

    def scattered(keep, send):
        for bit in bits[:-1]:
            came = flip(send, "tensor", tensor, bit)
            keep, send = fold(keep, came)
        return keep, flip(send, "tensor", tensor, bits[-1])

    def paired(keep, send):
        for bit in bits[:-2]:
            came = flip(send, "tensor", tensor, bit)
            keep, send = fold(keep, came)
        came = flip(send, "tensor", tensor, bits[-2])
        own, send = kernel_call(
            whole_fold_kernel, [(keep.shape, F32), (keep.shape, LOW)], keep, came
        )
        return own, flip(send, "tensor", tensor, bits[-1])

    def spread(rows):
        have = [rows]
        for bit in reversed(bits[:-1]):
            have += [flip(piece, "tensor", tensor, bit) for piece in have]
        return have

    def streams_of(count, orders):
        unit = 8 * dp * len(orders)
        padded = -(-count // unit) * unit
        return [(padded // len(orders), order) for order in orders]

    def two_grads(left_a, right_a, left_b, right_b, orders):
        streams = streams_of(left_a.shape[0] + left_b.shape[0], orders)
        outs = []
        for rows, _ in streams:
            outs += [((rows // 2, width), F32), ((rows // 2, width), LOW)]
        made = kernel_call(
            functools.partial(two_grads_kernel, streams=streams),
            outs,
            place,
            left_a,
            right_a,
            left_b,
            right_b,
            scratch=[pltpu.VMEM((sum(rows for rows, _ in streams), width), F32)],
            scalars=1,
            room=12,
        )
        return streams, made

    def dp_total(streams, made, count_a, count_b, gains=None):
        ends = []
        for at, (_, order) in enumerate(streams):
            keep, send = made[2 * at], made[2 * at + 1]
            for bit in order[:-2]:
                came = flip(send, "dp", dp, bit)
                keep, send = fold(keep, came)
            came = flip(send, "dp", dp, order[-2])
            riding = gains is not None and at == len(streams) - 1
            extra = 16 if riding else 0
            mine = kernel_call(
                exchange_fold_kernel,
                [((keep.shape[0] + extra, width), LOW)],
                keep,
                came,
                *([gains] if riding else []),
            )[0]
            came = flip(mine, "dp", dp, order[-1])
            mine = kernel_call(
                functools.partial(add_pair_kernel, extra=extra), [(mine.shape, LOW)], mine, came
            )[0]
            for bit in reversed(order[1:-1]):
                came = flip(mine, "dp", dp, bit)
                mine = kernel_call(
                    functools.partial(join_kernel, extra=extra),
                    [((2 * mine.shape[0] - extra, width), LOW)],
                    mine,
                    came,
                )[0]
            ends += [mine, flip(mine, "dp", dp, order[0])]
        return kernel_call(
            functools.partial(place_kernel, streams=streams, extra=gains is not None),
            [((count_a, width), F32), ((count_b, width), F32)]
            + ([((2, width), F32)] if gains is not None else []),
            place,
            *ends,
            scratch=[pltpu.VMEM((sum(rows for rows, _ in streams), width), F32)],
            scalars=1,
            room=12,
        )

    halves = [((half, width), F32), ((half, width), LOW)]
    qkv, probs, attended, first_low, keep, send = kernel_call(
        functools.partial(attend_kernel, pieces=tensor),
        [
            ((3 * feats, rows_all), LOW),
            ((heads, rows_all, rows_all), LOW),
            ((feats, rows_all), LOW),
            ((rows_all, width), LOW),
        ]
        + halves,
        *hidden_parts,
        gain1,
        qkv_rows,
        out_weight,
        cosine,
        sine,
        segments,
        room=16,
    )
    own, came = paired(keep, send)
    resid, second_own = kernel_call(
        second_norm_kernel,
        [(own.shape, F32), (own.shape, LOW)],
        *hidden_parts[:2],
        own,
        came,
        gain2,
    )
    grad_active, upstream = kernel_call(
        functools.partial(grad_active_kernel, pieces=tensor),
        [((units, rows_all), F32), ((rows_all, width), LOW)],
        *up_parts,
        down_weight,
        room=8,
    )
    second_parts = spread(second_own)
    second_low, active, grad_both, keep, send = kernel_call(
        functools.partial(forward_back_kernel, pieces=len(second_parts)),
        [((rows_all, width), LOW), ((units, rows_all), LOW), ((2 * units, rows_all), LOW)] + halves,
        *second_parts,
        in_rows,
        grad_active,
        room=12,
    )
    down_keep, down_send = kernel_call(down_kernel, halves, active, down_weight, room=8)
    out_own, out_came = scattered(down_keep, down_send)
    layer_out = kernel_call(add_kernel, [((rows_here, width), F32)], resid, out_own, out_came)[0]
    own, came = paired(keep, send)
    grad_resid, resid_own, norm2_part = kernel_call(
        resid_grad_kernel,
        [((rows_here, width), F32), (own.shape, LOW), ((1, width), F32)],
        *up_parts[:2],
        own,
        came,
        resid,
        gain2,
    )
    resid_parts = spread(resid_own)
    dp_bits = bits_of(dp)
    early_streams, early = two_grads(grad_both, second_low, active, upstream, early_orders(dp_bits))
    grad_in, grad_down = dp_total(early_streams, early, 2 * units, units)
    resid_low, grad_proj, keep, send = kernel_call(
        functools.partial(attend_back_kernel, pieces=len(resid_parts)),
        [((rows_all, width), LOW), ((3 * feats, rows_all), LOW)] + halves,
        *resid_parts,
        out_weight,
        qkv_rows,
        qkv,
        probs,
        attended,
        cosine,
        sine,
        room=16,
    )
    late_streams, late = two_grads(grad_proj, first_low, attended, resid_low, late_orders(dp_bits))
    own, came = scattered(keep, send)
    grad_input, gains = kernel_call(
        input_grad_kernel,
        [((rows_here, width), F32), ((2, width), F32)],
        own,
        came,
        hidden_in,
        gain1,
        grad_resid,
        norm2_part,
    )
    for bit in bits:
        came = flip(gains, "tensor", tensor, bit)
        gains = kernel_call(sum_kernel, [(gains.shape, F32)], gains, came)[0]
    grad_qkv, grad_out, gains = dp_total(late_streams, late, 3 * feats, feats, gains)
    return (
        layer_out,
        grad_input,
        grad_qkv.reshape(3, feats, width).transpose(2, 0, 1),
        grad_out,
        gains[0],
        grad_in.reshape(2, units, width).transpose(2, 0, 1),
        grad_down,
        gains[1],
    )


def solution(mesh):
    in_specs = (
        P(("dp", "tensor"), None),
        P("dp"),
        P(None, None, "tensor"),
        P("tensor", None),
        P(),
        P(None, None, "tensor"),
        P("tensor", None),
        P(),
        P(("dp", "tensor"), None),
    )
    out_specs = (
        P(("dp", "tensor"), None),
        P(("dp", "tensor"), None),
        P(None, None, "tensor"),
        P("tensor", None),
        P(),
        P(None, None, "tensor"),
        P("tensor", None),
        P(),
    )
    dp, tensor = mesh.shape["dp"], mesh.shape["tensor"]

    def run(*args):
        return body(*args, dp=dp, tensor=tensor)

    return jax.shard_map(run, mesh=mesh, in_specs=in_specs, out_specs=out_specs, check_vma=False)
```

```python
import functools
import math

import jax
import jax.numpy as jnp
from jax import lax
from jax.experimental import pallas as pl
from jax.experimental.pallas import tpu as pltpu
from jax.sharding import PartitionSpec as P


HD = 64
HALF = HD // 2
ROPE_LOG = math.log(160000.0)
EPS = 1e-05
FILL = -1e30
LOW = jnp.bfloat16
F32 = jnp.float32


def dot_nn(left, right):
    return lax.dot_general(left, right, (((1,), (0,)), ((), ())), preferred_element_type=F32)


def dot_nt(left, right):
    return lax.dot_general(left, right, (((1,), (1,)), ((), ())), preferred_element_type=F32)


def dot_tn(left, right):
    return lax.dot_general(left, right, (((0,), (0,)), ((), ())), preferred_element_type=F32)


def kernel_call(body, outs, *args, scratch=(), scalars=0, room=6, scalar_out=False, outside=0):
    shapes = [jax.ShapeDtypeStruct(shape, kind) for shape, kind in outs]
    specs = [pl.BlockSpec(memory_space=pltpu.SMEM)] * scalars
    specs += [pl.BlockSpec(memory_space=pltpu.VMEM)] * (len(args) - scalars - outside)
    specs += [pl.BlockSpec(memory_space=pltpu.HBM)] * outside
    out_specs = [pl.BlockSpec(memory_space=pltpu.VMEM)] * len(shapes)
    if scalar_out:
        out_specs[-1] = pl.BlockSpec(memory_space=pltpu.SMEM)
    inside = len(args) - outside
    args = args[:inside] + tuple(
        pltpu.with_memory_space_constraint(array, pltpu.HBM) for array in args[inside:]
    )
    return pl.pallas_call(
        body,
        out_shape=shapes,
        in_specs=specs,
        out_specs=out_specs,
        scratch_shapes=list(scratch),
        compiler_params=pltpu.CompilerParams(vmem_limit_bytes=room << 20),
    )(*args)


def offsets_of(bits):
    made = [0]
    for bit in reversed(bits):
        made = made + [at | bit for at in made]
    return made


def bits_of(size):
    return tuple(1 << at for at in range(size.bit_length() - 1))


def flip(value, axis_name, size, mask):
    return lax.ppermute(value, axis_name, [(at, at ^ mask) for at in range(size)])


def gather_rows(piece, size):
    have = {0: piece}
    for bit in reversed(bits_of(size)):
        for at in sorted(have):
            have[at | bit] = flip(have[at], "tensor", size, bit)
    return [have[at] for at in offsets_of(bits_of(size))]


def tables_kernel(spot, *refs, offsets, loads):
    sources, refs = refs[: loads + 3], refs[loads + 3 :]
    held, refs = refs[:loads], refs[loads:]
    cos_ref, sin_ref, seg_ref, gain1_ref, gain2_ref, place_ref, rows, seg, gain1, gain2, sems = refs
    copies = [
        pltpu.make_async_copy(source, target, sems.at[at])
        for at, (source, target) in enumerate(zip(sources, (seg, gain1, gain2) + tuple(held)))
    ]
    for copy in copies:
        copy.start()
    place_ref[0] = spot[1]
    for copy in copies[:3]:
        copy.wait()
    gain1_ref[...] = gain1[...].reshape(gain1_ref.shape)
    gain2_ref[...] = gain2[...].reshape(gain2_ref.shape)
    ids = seg[...].reshape(seg_ref.shape)
    count = ids.shape[1]
    lanes = lax.broadcasted_iota(jnp.int32, ids.shape, 1)
    before = jnp.where(lanes == 0, -1, pltpu.roll(ids, 1, 1))
    starts = jnp.where(ids != before, lanes, 0)
    reach = 1
    while reach < count:
        starts = jnp.maximum(starts, jnp.where(lanes >= reach, pltpu.roll(starts, reach, 1), 0))
        reach *= 2
    rows[0:1, :] = (lanes - starts).astype(F32)[0:1]
    rows[1:2, :] = ids.astype(F32)[0:1]
    step = count // len(offsets)
    turned = jnp.concatenate(
        [rows[:, pl.ds(pl.multiple_of((spot[0] ^ at) * step, step), step)] for at in offsets], 1
    )
    steps = lax.broadcasted_iota(jnp.int32, (HALF, count), 0).astype(F32)
    angles = jnp.exp(steps * (-2.0 / HD * ROPE_LOG)) * turned[0:1]
    cos_ref[...] = jnp.cos(angles)
    sin_ref[...] = jnp.sin(angles)
    seg_ref[...] = turned[1:2]
    for copy in copies[3:]:
        copy.wait()


def norm_rows(values, gain):
    centred = values - jnp.mean(values, -1, keepdims=True)
    scale_row = lax.rsqrt(jnp.mean(centred * centred, -1, keepdims=True) + EPS)
    normed = centred * scale_row
    return normed * gain, normed, scale_row


def norm_back(grad_out, normed, scale_row, gain):
    scaled = grad_out * gain
    return scale_row * (
        scaled
        - jnp.mean(scaled, -1, keepdims=True)
        - normed * jnp.mean(scaled * normed, -1, keepdims=True)
    )


def split_partial(partial, keep_ref, send_ref):
    half = partial.shape[0] // 2
    keep_ref[...] = partial[:half]
    send_ref[...] = partial[half:].astype(LOW)


def attend_kernel(*refs, pieces):
    parts = refs[:pieces]
    (gain, wqkv, wout, cosine, sine, seg, qkv_ref, p_ref, o_ref, h_ref, keep, send) = refs[pieces:]
    rows = jnp.concatenate([part[...] for part in parts], 0).astype(F32)
    first = norm_rows(rows, gain[...])[0].astype(LOW)
    h_ref[...] = first
    proj = dot_nt(wqkv[...], first)
    heads = wout.shape[0] // HD
    cos, sin = cosine[...], sine[...]
    made = []
    for at in range(2 * heads):
        upper = proj[at * HD : at * HD + HALF]
        lower = proj[at * HD + HALF : (at + 1) * HD]
        made += [upper * cos - lower * sin, lower * cos + upper * sin]
    made.append(proj[2 * heads * HD :])
    qkv_ref[...] = jnp.concatenate(made, 0).astype(LOW)
    count = seg.shape[1]
    row = seg[...]
    column = jnp.transpose(jnp.broadcast_to(row, (128, count)))[:, :1]
    same = column == row
    for head in range(heads):
        query = qkv_ref[head * HD : (head + 1) * HD, :]
        keys = qkv_ref[(heads + head) * HD : (heads + head + 1) * HD, :]
        values = qkv_ref[(2 * heads + head) * HD : (2 * heads + head + 1) * HD, :]
        scores = jnp.where(same, dot_tn(keys, query) * 0.125, FILL)
        top = jnp.max(scores, 0, keepdims=True)
        raised = jnp.exp(scores - top)
        total = jnp.sum(raised, 0, keepdims=True)
        probs = (raised * (1.0 / total)).astype(LOW)
        p_ref[head] = probs
        o_ref[head * HD : (head + 1) * HD, :] = dot_nn(values, probs).astype(LOW)
    split_partial(dot_tn(o_ref[...], wout[...]), keep, send)


def fold_kernel(keep, came, own_ref, send_ref):
    half = own_ref.shape[0]
    total = keep[...] + came[...].astype(F32)
    own_ref[...] = total[:half]
    send_ref[...] = total[half:].astype(LOW)


def whole_fold_kernel(keep, came, own_ref, send_ref):
    total = keep[...] + came[...].astype(F32)
    own_ref[...] = total
    send_ref[...] = total.astype(LOW)


def swapped(came):
    half = came.shape[0] // 2
    return jnp.concatenate([came[half:], came[:half]], 0).astype(F32)


def second_norm_kernel(*refs):
    own, came, gain, resid_ref, low_ref = refs[-5:]
    hidden = jnp.concatenate([part[...] for part in refs[:-5]], 0).astype(F32)
    resid = hidden + own[...] + swapped(came[...])
    resid_ref[...] = resid
    low_ref[...] = norm_rows(resid, gain[...])[0].astype(LOW)


def grad_active_kernel(*refs, pieces):
    down, da_ref, up_ref = refs[pieces:]
    rows = jnp.concatenate([part[...] for part in refs[:pieces]], 0)
    up_ref[...] = rows
    da_ref[...] = dot_nt(down[...], rows)


def forward_back_kernel(*refs, pieces):
    in_rows, grad_active, low_ref, active_ref, both_ref, keep, send = refs[pieces:]
    rows = jnp.concatenate([part[...] for part in refs[:pieces]], 0)
    low_ref[...] = rows
    both = dot_nt(in_rows[...], rows)
    hidden = both.shape[0] // 2
    gate, up = both[:hidden], both[hidden:]
    below = 0.5 * (1.0 + lax.erf(gate * (0.5**0.5)))
    bell = jnp.exp(-0.5 * gate * gate) * 0.3989422804014327
    active = gate * below
    active_ref[...] = (active * up).astype(LOW)
    came = grad_active[...]
    both_ref[:hidden, :] = (came * up * (below + gate * bell)).astype(LOW)
    both_ref[hidden:, :] = (came * active).astype(LOW)
    split_partial(dot_tn(both_ref[...], in_rows[...]), keep, send)


def down_kernel(active, down, keep, send):
    split_partial(dot_tn(active[...], down[...]), keep, send)


def emit_chunks(place, total, first, rows, keep, send, bits):
    offsets = offsets_of(bits)
    step = rows // len(offsets)
    half = len(offsets) // 2

    def chunk(offset):
        return total[pl.ds(pl.multiple_of(first + (place ^ offset) * step, 8), step), :]

    keep[...] = jnp.concatenate([chunk(at) for at in offsets[:half]], 0)
    send[...] = jnp.concatenate([chunk(at) for at in offsets[half:]], 0).astype(LOW)


def two_grads_kernel(place, left_a, right_a, left_b, right_b, *refs, streams):
    total = refs[-1]
    rows_a, rows_b = left_a.shape[0], left_b.shape[0]
    total[:rows_a, :] = dot_nn(left_a[...], right_a[...])
    total[rows_a : rows_a + rows_b, :] = dot_nn(left_b[...], right_b[...])
    spare = total.shape[0] - rows_a - rows_b
    if spare:
        total[rows_a + rows_b :, :] = jnp.zeros((spare, total.shape[1]), F32)
    first = 0
    for at, (rows, bits) in enumerate(streams):
        emit_chunks(place[0], total, first, rows, refs[2 * at], refs[2 * at + 1], bits)
        first += rows


def two_lows(values):
    high = values.astype(LOW).astype(F32)
    return jnp.concatenate([high, values - high, jnp.zeros((12, values.shape[1]), F32)], 0)


def gains_from(rows):
    return rows[0:2] + rows[2:4]


def exchange_fold_kernel(keep, came, *refs):
    total = keep[...] + came[...].astype(F32)
    if len(refs) == 2:
        total = jnp.concatenate([total, two_lows(refs[0][...])], 0)
    refs[-1][...] = total.astype(LOW)


def add_pair_kernel(mine, came, out_ref, *, extra):
    ours, theirs = mine[...].astype(F32), came[...].astype(F32)
    rows = ours.shape[0] - extra
    total = ours[:rows] + swapped(theirs[:rows])
    if extra:
        gains = gains_from(ours[rows:]) + gains_from(theirs[rows:])
        total = jnp.concatenate([total, two_lows(gains)], 0)
    out_ref[...] = total.astype(LOW)


def join_kernel(mine, came, out_ref, *, extra):
    ours, theirs = mine[...].astype(F32), came[...].astype(F32)
    rows = ours.shape[0] - extra
    parts = [ours[:rows], theirs[:rows]]
    if extra:
        parts.append(two_lows(gains_from(ours[rows:]) + gains_from(theirs[rows:])))
    out_ref[...] = jnp.concatenate(parts, 0).astype(LOW)


def place_kernel(place, *refs, streams, extra):
    inputs, outs, total = refs[: 2 * len(streams)], refs[2 * len(streams) : -1], refs[-1]
    first = 0
    for at, (rows, bits) in enumerate(streams):
        ours = inputs[2 * at][...].astype(F32)
        theirs = inputs[2 * at + 1][...].astype(F32)
        offsets = offsets_of(bits)
        step = rows // len(offsets)
        half = rows // 2
        for spot, offset in enumerate(offsets):
            source, begin = (ours, spot * step) if spot * step < half else (theirs, spot * step - half)
            start = pl.multiple_of(first + (place[0] ^ offset) * step, 8)
            total[pl.ds(start, step), :] = source[begin : begin + step]
        if extra and at == len(streams) - 1:
            gains = gains_from(ours[half:]) + gains_from(theirs[half:])
            outs[2][...] = gains[0:1].reshape(outs[2].shape)
            outs[3][...] = gains[1:2].reshape(outs[3].shape)
        first += rows
    rows_a, rows_b = outs[0].shape[0], outs[1].shape[0]
    outs[0][...] = total[:rows_a, :]
    outs[1][...] = total[rows_a : rows_a + rows_b, :]


def resid_grad_kernel(*refs):
    own, came, resid, gain, grad_ref, low_ref, gain_ref = refs[-7:]
    up = jnp.concatenate([part[...] for part in refs[:-7]], 0).astype(F32)
    _, normed, scale_row = norm_rows(resid[...], gain[...])
    grad_second = own[...] + swapped(came[...])
    grad = norm_back(grad_second, normed, scale_row, gain[...]) + up
    rows = grad_ref.shape[0]
    grad_ref[...] = grad[:rows]
    low_ref[...] = grad.astype(LOW)
    gain_ref[...] = jnp.sum(grad_second[:rows] * normed[:rows], 0, keepdims=True)


def attend_back_kernel(*refs, pieces):
    (wout, wqkv, qkv, probs, attended, cosine, sine, low_ref, dqkv_ref, keep, send) = refs[pieces:]
    rows = jnp.concatenate([part[...] for part in refs[:pieces]], 0)
    low_ref[...] = rows
    heads = wout.shape[0] // HD
    grad_att = dot_nt(wout[...], rows).astype(LOW)
    cos, sin = cosine[...], sine[...]
    made = [None] * (3 * heads)

    def turned_back(grad):
        upper, lower = grad[:HALF], grad[HALF:]
        return jnp.concatenate([upper * cos + lower * sin, lower * cos - upper * sin], 0)

    for head in range(heads):
        span = slice(head * HD, (head + 1) * HD)
        grad = grad_att[span]
        query = qkv[head * HD : (head + 1) * HD, :]
        keys = qkv[(heads + head) * HD : (heads + head + 1) * HD, :]
        values = qkv[(2 * heads + head) * HD : (2 * heads + head + 1) * HD, :]
        delta = jnp.sum(grad.astype(F32) * attended[span, :].astype(F32), 0, keepdims=True)
        low = probs[head]
        grad_probs = dot_tn(values, grad)
        grad_scores = (low.astype(F32) * (grad_probs - delta)).astype(LOW)
        made[head] = turned_back(dot_nn(keys, grad_scores) * 0.125)
        made[heads + head] = turned_back(dot_nt(query, grad_scores) * 0.125)
        made[2 * heads + head] = dot_nt(grad, low)
    dqkv_ref[...] = jnp.concatenate(made, 0).astype(LOW)
    split_partial(dot_tn(dqkv_ref[...], wqkv[...]), keep, send)


def input_grad_kernel(own, came, hidden, gain, resid_grad, gain2_part, grad_ref, gain_ref):
    _, normed, scale_row = norm_rows(hidden[...].astype(F32), gain[...])
    grad_first = own[...] + came[...].astype(F32)
    grad_ref[...] = norm_back(grad_first, normed, scale_row, gain[...]) + resid_grad[...]
    gain_ref[0:1, :] = jnp.sum(grad_first * normed, 0, keepdims=True)
    gain_ref[1:2, :] = gain2_part[...]


def add_kernel(resid, own, came, out_ref):
    out_ref[...] = resid[: out_ref.shape[0], :] + own[...] + came[...].astype(F32)


def sum_kernel(mine, came, out_ref):
    out_ref[...] = mine[...] + came[...]


def early_orders(bits):
    return (bits, bits)


def late_orders(bits):
    return (bits, bits)


def body(
    hidden_in,
    segment_ids,
    qkv_weight,
    out_weight,
    norm1_gain,
    in_weight,
    down_weight,
    norm2_gain,
    cotangent,
    *,
    dp,
    tensor,
):
    width = hidden_in.shape[1]
    rows_here = hidden_in.shape[0]
    rows_all = segment_ids.shape[0]
    feats = out_weight.shape[0]
    heads = feats // HD
    units = down_weight.shape[0]
    half = rows_all // 2
    qkv_rows = jnp.transpose(qkv_weight, (1, 2, 0)).reshape(3 * feats, width)
    in_rows = jnp.transpose(in_weight, (1, 2, 0)).reshape(2 * units, width)
    spot = jnp.stack([lax.axis_index("tensor"), lax.axis_index("dp")]).astype(jnp.int32)
    bits = bits_of(tensor)
    offsets = offsets_of(bits)
    hidden_parts = gather_rows(hidden_in, tensor)
    up_parts = gather_rows(cotangent, tensor)
    loads = [hidden_in, qkv_rows, out_weight, cotangent, down_weight, in_rows]
    *held, cosine, sine, segments, gain1, gain2, place = kernel_call(
        functools.partial(tables_kernel, offsets=offsets, loads=len(loads)),
        [(array.shape, array.dtype) for array in loads]
        + [((HALF, rows_all), F32), ((HALF, rows_all), F32), ((1, rows_all), F32)]
        + [((1, width), F32), ((1, width), F32), ((1,), jnp.int32)],
        spot,
        segment_ids,
        norm1_gain,
        norm2_gain,
        *loads,
        scratch=[
            pltpu.VMEM((2, rows_all), F32),
            pltpu.VMEM((rows_all,), jnp.int32),
            pltpu.VMEM((width,), F32),
            pltpu.VMEM((width,), F32),
            pltpu.SemaphoreType.DMA((len(loads) + 3,)),
        ],
        scalars=1,
        outside=len(loads) + 3,
        scalar_out=True,
    )
    hidden_in, qkv_rows, out_weight, cotangent, down_weight, in_rows = held
    hidden_parts[0] = hidden_in
    up_parts[0] = cotangent

    def fold(keep, came):
        rows = keep.shape[0] // 2
        return kernel_call(fold_kernel, [((rows, width), F32), ((rows, width), LOW)], keep, came)

    def scattered(keep, send):
        for bit in bits[:-1]:
            came = flip(send, "tensor", tensor, bit)
            keep, send = fold(keep, came)
        return keep, flip(send, "tensor", tensor, bits[-1])

    def paired(keep, send):
        for bit in bits[:-2]:
            came = flip(send, "tensor", tensor, bit)
            keep, send = fold(keep, came)
        came = flip(send, "tensor", tensor, bits[-2])
        own, send = kernel_call(
            whole_fold_kernel, [(keep.shape, F32), (keep.shape, LOW)], keep, came
        )
        return own, flip(send, "tensor", tensor, bits[-1])

    def spread(rows):
        have = [rows]
        for bit in reversed(bits[:-1]):
            have += [flip(piece, "tensor", tensor, bit) for piece in have]
        return have

    def streams_of(count, orders):
        unit = 8 * dp * len(orders)
        padded = -(-count // unit) * unit
        return [(padded // len(orders), order) for order in orders]

    def two_grads(left_a, right_a, left_b, right_b, orders):
        streams = streams_of(left_a.shape[0] + left_b.shape[0], orders)
        outs = []
        for rows, _ in streams:
            outs += [((rows // 2, width), F32), ((rows // 2, width), LOW)]
        made = kernel_call(
            functools.partial(two_grads_kernel, streams=streams),
            outs,
            place,
            left_a,
            right_a,
            left_b,
            right_b,
            scratch=[pltpu.VMEM((sum(rows for rows, _ in streams), width), F32)],
            scalars=1,
            room=12,
        )
        return streams, made

    def dp_total(streams, made, count_a, count_b, gains=None):
        ends = []
        for at, (_, order) in enumerate(streams):
            keep, send = made[2 * at], made[2 * at + 1]
            for bit in order[:-2]:
                came = flip(send, "dp", dp, bit)
                keep, send = fold(keep, came)
            came = flip(send, "dp", dp, order[-2])
            riding = gains is not None and at == len(streams) - 1
            extra = 16 if riding else 0
            mine = kernel_call(
                exchange_fold_kernel,
                [((keep.shape[0] + extra, width), LOW)],
                keep,
                came,
                *([gains] if riding else []),
            )[0]
            came = flip(mine, "dp", dp, order[-1])
            mine = kernel_call(
                functools.partial(add_pair_kernel, extra=extra), [(mine.shape, LOW)], mine, came
            )[0]
            for bit in reversed(order[1:-1]):
                came = flip(mine, "dp", dp, bit)
                mine = kernel_call(
                    functools.partial(join_kernel, extra=extra),
                    [((2 * mine.shape[0] - extra, width), LOW)],
                    mine,
                    came,
                )[0]
            ends += [mine, flip(mine, "dp", dp, order[0])]
        return kernel_call(
            functools.partial(place_kernel, streams=streams, extra=gains is not None),
            [((count_a, width), F32), ((count_b, width), F32)]
            + ([((width,), F32)] * 2 if gains is not None else []),
            place,
            *ends,
            scratch=[pltpu.VMEM((sum(rows for rows, _ in streams), width), F32)],
            scalars=1,
            room=12,
        )

    halves = [((half, width), F32), ((half, width), LOW)]
    qkv, probs, attended, first_low, keep, send = kernel_call(
        functools.partial(attend_kernel, pieces=tensor),
        [
            ((3 * feats, rows_all), LOW),
            ((heads, rows_all, rows_all), LOW),
            ((feats, rows_all), LOW),
            ((rows_all, width), LOW),
        ]
        + halves,
        *hidden_parts,
        gain1,
        qkv_rows,
        out_weight,
        cosine,
        sine,
        segments,
        room=16,
    )
    own, came = paired(keep, send)
    resid, second_own = kernel_call(
        second_norm_kernel,
        [(own.shape, F32), (own.shape, LOW)],
        *hidden_parts[:2],
        own,
        came,
        gain2,
    )
    grad_active, upstream = kernel_call(
        functools.partial(grad_active_kernel, pieces=tensor),
        [((units, rows_all), F32), ((rows_all, width), LOW)],
        *up_parts,
        down_weight,
        room=8,
    )
    second_parts = spread(second_own)
    second_low, active, grad_both, keep, send = kernel_call(
        functools.partial(forward_back_kernel, pieces=len(second_parts)),
        [((rows_all, width), LOW), ((units, rows_all), LOW), ((2 * units, rows_all), LOW)] + halves,
        *second_parts,
        in_rows,
        grad_active,
        room=12,
    )
    down_keep, down_send = kernel_call(down_kernel, halves, active, down_weight, room=8)
    out_own, out_came = scattered(down_keep, down_send)
    layer_out = kernel_call(add_kernel, [((rows_here, width), F32)], resid, out_own, out_came)[0]
    own, came = paired(keep, send)
    grad_resid, resid_own, norm2_part = kernel_call(
        resid_grad_kernel,
        [((rows_here, width), F32), (own.shape, LOW), ((1, width), F32)],
        *up_parts[:2],
        own,
        came,
        resid,
        gain2,
    )
    resid_parts = spread(resid_own)
    dp_bits = bits_of(dp)
    early_streams, early = two_grads(grad_both, second_low, active, upstream, early_orders(dp_bits))
    grad_in, grad_down = dp_total(early_streams, early, 2 * units, units)
    resid_low, grad_proj, keep, send = kernel_call(
        functools.partial(attend_back_kernel, pieces=len(resid_parts)),
        [((rows_all, width), LOW), ((3 * feats, rows_all), LOW)] + halves,
        *resid_parts,
        out_weight,
        qkv_rows,
        qkv,
        probs,
        attended,
        cosine,
        sine,
        room=16,
    )
    late_streams, late = two_grads(grad_proj, first_low, attended, resid_low, late_orders(dp_bits))
    own, came = scattered(keep, send)
    grad_input, gains = kernel_call(
        input_grad_kernel,
        [((rows_here, width), F32), ((2, width), F32)],
        own,
        came,
        hidden_in,
        gain1,
        grad_resid,
        norm2_part,
    )
    for bit in bits:
        came = flip(gains, "tensor", tensor, bit)
        gains = kernel_call(sum_kernel, [(gains.shape, F32)], gains, came)[0]
    grad_qkv, grad_out, grad_norm1, grad_norm2 = dp_total(late_streams, late, 3 * feats, feats, gains)
    return (
        layer_out,
        grad_input,
        grad_qkv.reshape(3, feats, width).transpose(2, 0, 1),
        grad_out,
        grad_norm1,
        grad_in.reshape(2, units, width).transpose(2, 0, 1),
        grad_down,
        grad_norm2,
    )


def solution(mesh):
    in_specs = (
        P(("dp", "tensor"), None),
        P("dp"),
        P(None, None, "tensor"),
        P("tensor", None),
        P(),
        P(None, None, "tensor"),
        P("tensor", None),
        P(),
        P(("dp", "tensor"), None),
    )
    out_specs = (
        P(("dp", "tensor"), None),
        P(("dp", "tensor"), None),
        P(None, None, "tensor"),
        P("tensor", None),
        P(),
        P(None, None, "tensor"),
        P("tensor", None),
        P(),
    )
    dp, tensor = mesh.shape["dp"], mesh.shape["tensor"]

    def run(*args):
        return body(*args, dp=dp, tensor=tensor)

    return jax.shard_map(run, mesh=mesh, in_specs=in_specs, out_specs=out_specs, check_vma=False)
```
